32 devices in a mesh: pb: 8 (over y, x, core), dev: 4 (over z).
Axes of the slice: x: 2, y: 2, z: 4, core: 2. Of those that a mesh axis runs over, the one named last changes fastest.
Arguments:
- query_factors: float32 [8192, 128], P('pb'), may hold values from -2.4 to 2.4
- panel_factors: float32 [8192, 128], P(('pb', 'dev')), may hold values from -2.4 to 2.4
- query_weight: float32 [8192], P('pb'), may hold values from 1 to 144, as said below
- plan: int32 [8], replicated, may hold values from 0 to 7, each once
- tile_seeds: int32 [8, 8], replicated, may hold values from 0 to 65520
Outputs:
- query_out: float32 [8192, 128], P('pb')
- panel_out: float32 [8192, 128], P(('pb', 'dev'))
The draws below stay inside these ranges and needn't reach their ends.
Inputs may be any that keep to these rules, and one draw needn't show every extreme that they name: `query_weight`: each row's weight is positive and at most 144.
All inputs are finite; a program needn't handle non-finite values.
Results may differ from the reference program's by a relative error of at most 0.00018.
Values sent between devices are 32-bit elements; how exact they have to be, the bound alone decides.
No kernel may reach another device: no remote copies, remote signals or barrier semaphores. Data moves between devices by JAX's collectives and lax.ppermute only.
A program may use at most 64 MiB of HBM per device.

```python
import math
import jax
import jax.numpy as jnp
from jax import lax

QB = 1024
DC = 256
K = 128
STRATA = 3
PANELS = 8
QUERIES = 8192
DOCS = 8192
N_DEV = 4


def draw_query_weight(key, part):
    row_pos = jnp.arange(QUERIES, dtype=jnp.float32) / max(QUERIES - 1, 1)
    spread_log = jax.random.uniform(key, (QUERIES,), jnp.float32, 0.0, math.log(10.0))
    rising = 3.0 ** row_pos
    return (jnp.exp(spread_log) * rising).astype(jnp.float32)


def plant(entries, rng, low, high):
    shape = entries.shape
    place = [jax.random.randint(jax.random.fold_in(rng, axis), (), 0, shape[axis]) for axis in range(len(shape))]
    entries = entries.at[tuple(place)].set(low)
    longest = shape.index(max(shape))
    place[longest] = (place[longest] + 1) % shape[longest]
    return entries.at[tuple(place)].set(high)


def block_scale(rng, shape, cuts, least, largest):
    factor_of, own = 1.0, jax.random.fold_in(rng, 6)
    for axis_at, shards_of in cuts:
        heights = jnp.exp(jax.random.uniform(jax.random.fold_in(own, axis_at), (shards_of,), jnp.float32, least / len(cuts), largest / len(cuts)))
        factor_of = factor_of * jnp.repeat(heights, shape[axis_at] // shards_of).reshape([-1 if axis == axis_at else 1 for axis in range(len(shape))])
    return factor_of


def scatter_about(rng, shape, scale, reach, split=(), held_as=jnp.bfloat16):
    level = block_scale(rng, shape, split, -0.22, 0.18) if split else 1.0
    values = jax.random.normal(rng, shape, jnp.float32) * scale * level
    return jnp.minimum(jnp.maximum(values, -reach), reach).astype(held_as)


def setup_inputs(seed: int = 0) -> dict:
    arg_keys = jax.random.split(jax.random.key(seed), 6)
    return {
        "query_factors": scatter_about(arg_keys[0], (QUERIES, K), 0.3, 2.4, ((0, 8),), jnp.float32),
        "panel_factors": scatter_about(arg_keys[1], (DOCS, K), 0.3, 2.4, ((0, 32),), jnp.float32),
        "query_weight": draw_query_weight(jax.random.fold_in(arg_keys[5], 71), 0),
        "plan": jax.random.permutation(arg_keys[3], PANELS).astype(jnp.int32),
        "tile_seeds": plant(jax.random.randint(arg_keys[4], (PANELS, PANELS), 0, 65521), jax.random.fold_in(arg_keys[4], 1), 0, 65520).astype(jnp.int32),
    }


epsilon = 1e-06
learning_rate = 0.3

def shift_down(mixed, count):
    return lax.shift_right_logical(mixed, jnp.full(mixed.shape, count, jnp.int32))

def hashed(tile_seed, row_ids, col_ids):
    mixed = tile_seed * 374761393 + row_ids * 668265263 + col_ids * 1274126177
    mixed = mixed ^ shift_down(mixed, 15)
    mixed = mixed * 73244475
    mixed = mixed ^ shift_down(mixed, 13)
    mixed = mixed * 1911520717
    mixed = mixed ^ shift_down(mixed, 16)
    return (mixed & 65535).astype(jnp.float32) / 32768.0 - 1.0

def reference(query_factors, panel_factors, query_weight, plan, tile_seeds):
    groups = PANELS
    width = N_DEV * DC
    factors = query_factors.reshape(groups, QB, K)
    panels = panel_factors.reshape(groups, width, K)
    weights = query_weight.reshape(groups, QB)
    positions = jnp.arange(groups, dtype=jnp.int32)
    local_rows = jnp.arange(QB, dtype=jnp.int32)[:, None]
    local_cols = jnp.arange(width, dtype=jnp.int32)[None, :]
    for stratum in range(STRATA):
        panel_ids = plan[jnp.mod(positions - stratum, groups)]
        seed_list = tile_seeds[positions, panel_ids]

        def one_block(items):
            block_u, block_v, block_w, position, panel_id, tile_seed = items
            scores = hashed(tile_seed, position * QB + local_rows, panel_id * width + local_cols)
            approx = jnp.dot(block_u, block_v.T, precision=lax.Precision.HIGHEST)
            weighted = block_w[:, None] * (scores - approx)
            grad_u = jnp.dot(weighted, block_v, precision=lax.Precision.HIGHEST)
            grad_v = jnp.dot(weighted.T, block_u, precision=lax.Precision.HIGHEST)
            return (grad_u, grad_v)
        grad_u, grad_v = lax.map(one_block, (factors, panels, weights, positions, panel_ids, seed_list))
        factors = factors + learning_rate * grad_u / jnp.sqrt(jnp.mean(grad_u * grad_u) + epsilon)
        panels = panels + learning_rate * grad_v / jnp.sqrt(jnp.mean(grad_v * grad_v) + epsilon)
        panels = jnp.roll(panels, 1, axis=0)
    return (factors.reshape(QUERIES, K), panels.reshape(DOCS, K))
```

```python
import functools

import jax
import jax.numpy as jnp
from jax import lax
from jax.experimental import pallas as pl
from jax.experimental.pallas import tpu as pltpu
from jax.sharding import PartitionSpec as P

STRATA = 3
epsilon = 1e-06
learning_rate = 0.3


SMEM = pl.BlockSpec(memory_space=pltpu.SMEM)
VMEM = pl.BlockSpec(memory_space=pltpu.VMEM)
f32, bf16 = jnp.float32, jnp.bfloat16


def dot(a, b):
    return jnp.dot(a, b, preferred_element_type=f32)


def pieces(x):
    hi = x.astype(bf16)
    return hi, (x - hi.astype(f32)).astype(bf16)


def call(kernel, out_shape, operands, in_specs=None, scratch=(), flops=0, moved=0):
    return pl.pallas_call(
        kernel,
        out_shape=out_shape,
        in_specs=in_specs or [VMEM] * len(operands),
        out_specs=jax.tree.map(lambda _: VMEM, out_shape),
        scratch_shapes=list(scratch),
        compiler_params=pltpu.CompilerParams(vmem_limit_bytes=60 << 20),
        cost_estimate=pl.CostEstimate(flops=flops, bytes_accessed=moved, transcendentals=0),
    )(*operands)


def hash_kernel(stratum, plan_ref, seeds_ref, first_ref, second_ref):
    rows, cols = first_ref.shape
    groups = plan_ref.shape[0]
    position = lax.axis_index("pb")
    panel_id = plan_ref[lax.rem(position + (STRATA * groups - stratum), groups)]
    base = (
        seeds_ref[position, panel_id] * 374761393
        + (position * rows) * 668265263
        + (panel_id * cols) * 1274126177
    )
    step, width = 32, min(cols, 512)
    local_rows = lax.broadcasted_iota(jnp.int32, (step, width), 0)
    local_cols = lax.broadcasted_iota(jnp.int32, (step, width), 1)
    offsets = local_rows * 668265263 + local_cols * 1274126177

    def strip(k, _):
        row = pl.multiple_of(k * step, step)
        for col in range(0, cols, width):
            mixed = offsets + (base + row * 668265263 + jnp.int32(col) * 1274126177)
            mixed = mixed ^ lax.shift_right_logical(mixed, jnp.full(mixed.shape, 15, jnp.int32))
            mixed = mixed * 73244475
            mixed = mixed ^ lax.shift_right_logical(mixed, jnp.full(mixed.shape, 13, jnp.int32))
            mixed = mixed * 1911520717
            mixed = mixed ^ lax.shift_right_logical(mixed, jnp.full(mixed.shape, 16, jnp.int32))
            high = lax.shift_right_logical(mixed, jnp.full(mixed.shape, 8, jnp.int32)) & 255
            low = mixed & 255
            first_ref[pl.ds(row, step), pl.ds(col, width)] = (
                high.astype(f32) * (1 / 128) - 1.0
            ).astype(bf16)
            second_ref[pl.ds(row, step), pl.ds(col, width)] = (
                low.astype(f32) * (1 / 32768)
            ).astype(bf16)
        return 0

    lax.fori_loop(0, rows // step, strip, 0)


def step_size(tile, count):
    return learning_rate / jnp.sqrt(
        jnp.sum(tile, axis=(0, 1), keepdims=True) / count + epsilon
    )


def times_gram(left, gram):
    k = gram.shape[0]
    high, low = pieces(gram)
    left_high, left_low = pieces(left)
    packed = jnp.concatenate([left_high, left_low], axis=1)
    wide = jnp.concatenate(
        [
            jnp.concatenate([high, low], axis=1),
            jnp.concatenate([high, jnp.zeros_like(low)], axis=1),
        ],
        axis=0,
    )
    out = dot(packed, wide)
    return out[:, :k] + out[:, k:]


def fold(square):
    k = square.shape[0] // 2
    return square[:k, :k] + (square[:k, k:] + square[k:, :k])


def query_kernel(count, *refs):
    if count is None:
        factors_ref, weight_ref, first_ref, second_ref, p_ref, gram_ref = refs
        factors = factors_ref[...]
    else:
        (before_ref, grad_ref, sums_ref, weight_ref, first_ref, second_ref,
         factors_ref, p_ref, gram_ref) = refs
        factors = before_ref[...] + step_size(sums_ref[:8, :], count) * grad_ref[...]
        factors_ref[...] = factors
    k = factors.shape[1]
    scaled = (weight_ref[...] * factors).T
    high, low = pieces(scaled)
    scaled = jnp.concatenate([high, low], axis=0)
    gram_ref[...] = fold(dot(scaled, jnp.concatenate(pieces(factors), axis=1)))
    cols = first_ref.shape[1]
    width = 256

    def strip(j, _):
        at = pl.ds(pl.multiple_of(j * width, width), width)
        out = dot(scaled, first_ref[:, at]) + dot(scaled, second_ref[:, at])
        p_ref[at, :] = (out[:k] + out[k:]).T
        return 0

    lax.fori_loop(0, cols // width, strip, 0)


def add_squares(ref, row, block):
    rows, k = block.shape
    ref[row : row + 8, :] += jnp.sum((block * block).reshape(rows // 8, 8, k), axis=0)


def panel_kernel(stratum, count, parts, *refs):
    refs = list(refs)
    last = stratum == STRATA - 1
    if stratum == 0:
        panel_parts, refs = refs[:parts], refs[parts:]
    else:
        before_ref, step_ref, sums_ref = refs[:3]
        refs = refs[3:]
    factors_ref, weight_ref, first_ref, second_ref, p_ref, gram_ref = refs[:6]
    grad_ref, out_v_ref, out_h_ref, squares_ref = refs[6:10]
    panel_ref, h_ref, packed_ref = refs[10:] if last else (out_v_ref, out_h_ref, refs[10])
    rows, k = factors_ref.shape
    cols = first_ref.shape[1]
    if stratum == 0:
        own = lax.axis_index("dev")
        each = panel_parts[0].shape[0]
        for i, part in enumerate(panel_parts):
            place = pl.multiple_of((own ^ i) * each, each) if parts > 1 else 0
            panel_ref[pl.ds(place, each), :] = part[...]
    else:
        panel_ref[...] = before_ref[...] + step_size(sums_ref[8:, :], count) * step_ref[...]
    squares_ref[...] = jnp.zeros_like(squares_ref)
    panel = panel_ref[...]
    packed_ref[...] = jnp.concatenate(pieces(panel), axis=1)
    packed = packed_ref[...]
    h = p_ref[...] - times_gram(panel, gram_ref[...])
    h_ref[...] = h
    add_squares(squares_ref, 8, h)
    panel_gram = fold(
        lax.dot_general(packed, packed, (((0,), (0,)), ((), ())), preferred_element_type=f32)
    )
    height = 256

    def strip(j, _):
        at = pl.ds(pl.multiple_of(j * height, height), height)
        out = dot(first_ref[at, :], packed_ref[...]) + dot(second_ref[at, :], packed_ref[...])
        g = weight_ref[at, :] * (
            (out[:, :k] + out[:, k:]) - times_gram(factors_ref[at, :], panel_gram)
        )
        grad_ref[at, :] = g
        add_squares(squares_ref, 0, g)
        return 0

    lax.fori_loop(0, rows // height, strip, 0)
    if last:
        each = out_v_ref.shape[0]
        own = lax.axis_index("dev")
        at = pl.ds(pl.multiple_of(own * each, each), each)
        out_v_ref[...] = panel_ref[at, :]
        out_h_ref[...] = h_ref[at, :]


def last_kernel(u_count, v_count, u_ref, g_ref, v_ref, h_ref, sums_ref, u_out, v_out):
    u_out[...] = u_ref[...] + step_size(sums_ref[:8, :], u_count) * g_ref[...]
    v_out[...] = v_ref[...] + step_size(sums_ref[8:, :], v_count) * h_ref[...]


def shifted(array, axis, by):
    size = lax.axis_size(axis)
    return lax.ppermute(array, axis, [(i, (i + by) % size) for i in range(size)])


def crossed(array, axis, mask):
    return lax.ppermute(array, axis, [(i, i ^ mask) for i in range(lax.axis_size(axis))])


def power_of_two(size):
    return size & (size - 1) == 0


def summed(tile, axis):
    size = lax.axis_size(axis)
    if not power_of_two(size):
        return lax.psum(tile, axis)
    if size > 1:
        tile = tile + crossed(tile, axis, 1)
    at = 2
    while at < size:
        if 2 * at < size:
            tile = (tile + crossed(tile, axis, at)) + (
                crossed(tile, axis, 2 * at) + crossed(tile, axis, 3 * at)
            )
            at *= 4
        else:
            tile = tile + crossed(tile, axis, at)
            at *= 2
    return tile


def per_device(query_factors, panel_factors, query_weight, plan, tile_seeds):
    groups = lax.axis_size("pb")
    spread = lax.axis_size("dev")
    rows, k = query_factors.shape
    each = panel_factors.shape[0]
    cols = each * spread
    u_count = float(rows * groups * k)
    v_count = float(cols * groups * k)
    weight = query_weight[:, None]
    shape = jax.ShapeDtypeStruct
    work = 2 * rows * cols * k

    scores = [
        call(
            functools.partial(hash_kernel, t),
            [shape((rows, cols), bf16)] * 2,
            (plan, tile_seeds),
            in_specs=[SMEM, SMEM],
            flops=rows * cols * 20,
            moved=4 * rows * cols,
        )
        for t in range(STRATA)
    ]
    if spread <= 4 and power_of_two(spread):
        parts = [panel_factors] + [crossed(panel_factors, "dev", i) for i in range(1, spread)]
    else:
        parts = [lax.all_gather(panel_factors, "dev", axis=0, tiled=True)]

    factors, grad, sums, panel_in = query_factors, None, None, parts
    for t in range(STRATA):
        last = t == STRATA - 1
        outs = [shape((cols, k), f32), shape((k, k), f32)]
        if t == 0:
            p, gram = call(
                functools.partial(query_kernel, None), outs,
                (factors, weight, *scores[t]), flops=4 * work, moved=4 * rows * cols,
            )
        else:
            factors, p, gram = call(
                functools.partial(query_kernel, u_count), [shape((rows, k), f32)] + outs,
                (factors, grad, sums, weight, *scores[t]), flops=4 * work, moved=4 * rows * cols,
            )
            panel_in = [panel_in[0], panel_in[1], sums]
        held = each if last else cols
        scratch = [pltpu.VMEM((cols, 2 * k), bf16)]
        if last:
            scratch = [pltpu.VMEM((cols, k), f32)] * 2 + scratch
        grad, panel, grad_v, squares = call(
            functools.partial(panel_kernel, t, v_count, len(parts)),
            [shape((rows, k), f32), shape((held, k), f32), shape((held, k), f32), shape((16, k), f32)],
            (*panel_in, factors, weight, *scores[t], p, gram),
            scratch=scratch, flops=4 * work, moved=4 * rows * cols,
        )
        sums = summed(squares, "pb")
        panel_in = [shifted(panel, "pb", 1), shifted(grad_v, "pb", 1)]
    return call(
        functools.partial(last_kernel, u_count, v_count),
        [shape((rows, k), f32), shape((each, k), f32)],
        (factors, grad, *panel_in, sums),
    )


def solution(mesh):
    return jax.shard_map(
        lambda *args: tuple(per_device(*args)),
        mesh=mesh,
        in_specs=(P("pb", None), P(("pb", "dev"), None), P("pb"), P(), P()),
        out_specs=(P("pb", None), P(("pb", "dev"), None)),
        check_vma=False,
    )
```

```python
import functools

import jax
import jax.numpy as jnp
from jax import lax
from jax.experimental import pallas as pl
from jax.experimental.pallas import tpu as pltpu
from jax.sharding import PartitionSpec as P

STRATA = 3
epsilon = 1e-06
learning_rate = 0.3


SMEM = pl.BlockSpec(memory_space=pltpu.SMEM)
VMEM = pl.BlockSpec(memory_space=pltpu.VMEM)
f32, bf16 = jnp.float32, jnp.bfloat16


def dot(a, b):
    return jnp.dot(a, b, preferred_element_type=f32)


def pieces(x):
    hi = x.astype(bf16)
    return hi, (x - hi.astype(f32)).astype(bf16)


def call(kernel, out_shape, operands, limit, in_specs=None, scratch=(), flops=0, moved=0):
    return pl.pallas_call(
        kernel,
        out_shape=out_shape,
        in_specs=in_specs or [VMEM] * len(operands),
        out_specs=jax.tree.map(lambda _: VMEM, out_shape),
        scratch_shapes=list(scratch),
        compiler_params=pltpu.CompilerParams(vmem_limit_bytes=limit),
        cost_estimate=pl.CostEstimate(flops=flops, bytes_accessed=moved, transcendentals=0),
    )(*operands)


def hash_kernel(stratum, plan_ref, seeds_ref, first_ref, second_ref):
    rows, cols = first_ref.shape
    groups = plan_ref.shape[0]
    position = lax.axis_index("pb")
    panel_id = plan_ref[lax.rem(position + (STRATA * groups - stratum), groups)]
    base = (
        seeds_ref[position, panel_id] * 374761393
        + (position * rows) * 668265263
        + (panel_id * cols) * 1274126177
    )
    step, width = 32, min(cols, 512)
    local_rows = lax.broadcasted_iota(jnp.int32, (step, width), 0)
    local_cols = lax.broadcasted_iota(jnp.int32, (step, width), 1)
    offsets = local_rows * 668265263 + local_cols * 1274126177

    def strip(k, _):
        row = pl.multiple_of(k * step, step)
        for col in range(0, cols, width):
            mixed = offsets + (base + row * 668265263 + jnp.int32(col) * 1274126177)
            mixed = mixed ^ lax.shift_right_logical(mixed, jnp.full(mixed.shape, 15, jnp.int32))
            mixed = mixed * 73244475
            mixed = mixed ^ lax.shift_right_logical(mixed, jnp.full(mixed.shape, 13, jnp.int32))
            mixed = mixed * 1911520717
            mixed = mixed ^ lax.shift_right_logical(mixed, jnp.full(mixed.shape, 16, jnp.int32))
            first_ref[pl.ds(row, step), pl.ds(col, width)] = (
                (mixed & 65280).astype(f32) - 32768.0
            ).astype(bf16)
            second_ref[pl.ds(row, step), pl.ds(col, width)] = (
                (mixed & 255).astype(f32).astype(bf16)
            )
        return 0

    lax.fori_loop(0, rows // step, strip, 0)


def step_size(tiles, row, count):
    tile = functools.reduce(jnp.add, [ref[row : row + 8, :] for ref in tiles])
    return learning_rate / jnp.sqrt(
        jnp.sum(tile, axis=(0, 1), keepdims=True) / count + epsilon
    )


def times_gram(left, gram):
    k = gram.shape[0]
    high, low = pieces(gram)
    left_high, left_low = pieces(left)
    packed = jnp.concatenate([left_high, left_low], axis=1)
    wide = jnp.concatenate(
        [
            jnp.concatenate([high, low], axis=1),
            jnp.concatenate([high, jnp.zeros_like(low)], axis=1),
        ],
        axis=0,
    )
    out = dot(packed, wide)
    return out[:, :k] + out[:, k:]


def fold(square):
    k = square.shape[0] // 2
    return square[:k, :k] + (square[:k, k:] + square[k:, :k])


def add_squares(ref, row, block):
    rows, k = block.shape
    ref[row : row + 8, :] += jnp.sum((block * block).reshape(rows // 8, 8, k), axis=0)


def weight_kernel(weight_ref, out_ref):
    strips, k = weight_ref.shape
    for i in range(strips):
        out_ref[i * k : (i + 1) * k, :] = jnp.broadcast_to(weight_ref[i : i + 1, :], (k, k)).T


def query_side(factors, weight, first_ref, second_ref, p_ref, gram_ref, packed_ref):
    k = factors.shape[1]
    scaled = (weight * factors).T
    packed = jnp.concatenate(pieces(scaled), axis=0)
    gram_ref[...] = fold(dot(packed, jnp.concatenate(pieces(factors), axis=1)))
    packed_ref[...] = packed * jnp.asarray(1 / 32768, bf16)
    cols = first_ref.shape[1]
    width = 256

    def strip(j, _):
        at = pl.ds(pl.multiple_of(j * width, width), width)
        out = dot(packed_ref[...], first_ref[:, at]) + dot(packed_ref[...], second_ref[:, at])
        p_ref[at, :] = (out[:k] + out[k:]).T
        return 0

    lax.fori_loop(0, cols // width, strip, 0)


def panel_side(panel, factors_ref, weight_ref, first_ref, second_ref, p_ref, gram,
               grad_ref, h_ref, squares_ref, packed_ref):
    rows, k = factors_ref.shape
    squares_ref[...] = jnp.zeros_like(squares_ref)
    packed = jnp.concatenate(pieces(panel), axis=1)
    packed_ref[...] = packed * jnp.asarray(1 / 32768, bf16)
    h = p_ref[...] - times_gram(panel, gram)
    h_ref[...] = h
    add_squares(squares_ref, 8, h)
    panel_gram = fold(
        lax.dot_general(packed, packed, (((0,), (0,)), ((), ())), preferred_element_type=f32)
    )
    height = 256

    def strip(j, _):
        at = pl.ds(pl.multiple_of(j * height, height), height)
        out = dot(first_ref[at, :], packed_ref[...]) + dot(second_ref[at, :], packed_ref[...])
        g = weight_ref[at, :] * (
            (out[:, :k] + out[:, k:]) - times_gram(factors_ref[at, :], panel_gram)
        )
        grad_ref[at, :] = g
        add_squares(squares_ref, 0, g)
        return 0

    lax.fori_loop(0, rows // height, strip, 0)


def query_kernel(factors_ref, weight_ref, first_ref, second_ref, p_ref, gram_ref, scaled_ref):
    query_side(factors_ref[...], weight_ref[...], first_ref, second_ref, p_ref, gram_ref, scaled_ref)


def panel_kernel(*refs):
    panel_parts, refs = refs[:-11], refs[-11:]
    (factors_ref, weight_ref, first_ref, second_ref, p_ref, gram_ref,
     grad_ref, panel_ref, h_ref, squares_ref, packed_ref) = refs
    own = lax.axis_index("dev")
    each = panel_parts[0].shape[0]
    for i, part in enumerate(panel_parts):
        place = pl.multiple_of((own ^ i) * each, each) if len(panel_parts) > 1 else 0
        panel_ref[pl.ds(place, each), :] = part[...]
    panel_side(panel_ref[...], factors_ref, weight_ref, first_ref, second_ref, p_ref,
               gram_ref[...], grad_ref, h_ref, squares_ref, packed_ref)


def stratum_kernel(last, u_count, v_count, *refs):
    refs = list(refs)
    u_before, g_before, v_before, h_before, weight_ref, first_ref, second_ref = refs[:7]
    rest = 11 if last else 9
    tiles, refs = refs[7:-rest], refs[-rest:]
    factors_ref, grad_ref, v_out, h_out, squares_ref, p_ref, gram_ref, packed_ref, scaled_ref = refs[:9]
    factors = u_before[...] + step_size(tiles, 0, u_count) * g_before[...]
    factors_ref[...] = factors
    panel = v_before[...] + step_size(tiles, 8, v_count) * h_before[...]
    panel_ref, h_ref = refs[9:] if last else (v_out, h_out)
    panel_ref[...] = panel
    query_side(factors, weight_ref[...], first_ref, second_ref, p_ref, gram_ref, scaled_ref)
    panel_side(panel, factors_ref, weight_ref, first_ref, second_ref, p_ref, gram_ref[...],
               grad_ref, h_ref, squares_ref, packed_ref)
    if last:
        each = v_out.shape[0]
        at = pl.ds(pl.multiple_of(lax.axis_index("dev") * each, each), each)
        v_out[...] = panel_ref[at, :]
        h_out[...] = h_ref[at, :]


def last_kernel(u_count, v_count, u_ref, g_ref, v_ref, h_ref, *refs):
    tiles, (u_out, v_out) = refs[:-2], refs[-2:]
    u_out[...] = u_ref[...] + step_size(tiles, 0, u_count) * g_ref[...]
    v_out[...] = v_ref[...] + step_size(tiles, 8, v_count) * h_ref[...]


def shifted(array, axis, by):
    size = lax.axis_size(axis)
    return lax.ppermute(array, axis, [(i, (i + by) % size) for i in range(size)])


def crossed(array, axis, mask):
    return lax.ppermute(array, axis, [(i, i ^ mask) for i in range(lax.axis_size(axis))])


def power_of_two(size):
    return size & (size - 1) == 0


def summands(tile, axis):
    size = lax.axis_size(axis)
    if not power_of_two(size):
        return [lax.psum(tile, axis)]
    tiles, at = [tile], 1
    while at < size:
        tile = functools.reduce(jnp.add, tiles)
        span = 3 if at > 1 and 2 * at < size else 1
        tiles = [tile] + [crossed(tile, axis, at * i) for i in range(1, span + 1)]
        at *= span + 1
    return tiles


def per_device(query_factors, panel_factors, query_weight, plan, tile_seeds):
    groups = lax.axis_size("pb")
    spread = lax.axis_size("dev")
    rows, k = query_factors.shape
    each = panel_factors.shape[0]
    cols = each * spread
    u_count = float(rows * groups * k)
    v_count = float(cols * groups * k)
    shape = jax.ShapeDtypeStruct
    work = 2 * rows * cols * k
    limit = (6 << 20) + 4 * rows * cols + 28 * k * (rows + cols)
    tile = shape((rows, k), f32)
    whole = shape((cols, k), f32)
    squares = shape((16, k), f32)
    across = pltpu.VMEM((2 * k, rows), bf16)
    pack = pltpu.VMEM((cols, 2 * k), bf16)

    scores = [
        call(
            functools.partial(hash_kernel, t),
            [shape((rows, cols), bf16)] * 2,
            (plan, tile_seeds),
            limit,
            in_specs=[SMEM, SMEM],
            flops=rows * cols * 20,
            moved=4 * rows * cols,
        )
        for t in range(STRATA)
    ]
    weight = call(weight_kernel, [tile], (query_weight.reshape(rows // k, k),), limit)[0]
    if spread <= 4 and power_of_two(spread):
        parts = [panel_factors] + [crossed(panel_factors, "dev", i) for i in range(1, spread)]
    else:
        parts = [lax.all_gather(panel_factors, "dev", axis=0, tiled=True)]
    factors = query_factors
    p, gram = call(
        query_kernel, [whole, shape((k, k), f32)], (factors, weight, *scores[0]), limit,
        scratch=[across], flops=4 * work, moved=4 * rows * cols,
    )
    grad, panel, grad_v, sums = call(
        panel_kernel, [tile, whole, whole, squares],
        (*parts, factors, weight, *scores[0], p, gram), limit,
        scratch=[pack], flops=4 * work, moved=4 * rows * cols,
    )
    for t in range(1, STRATA):
        tiles = summands(sums, "pb")
        panel, grad_v = shifted(panel, "pb", 1), shifted(grad_v, "pb", 1)
        last = t == STRATA - 1
        kept = shape((each, k), f32) if last else whole
        factors, grad, panel, grad_v, sums = call(
            functools.partial(stratum_kernel, last, u_count, v_count),
            [tile, tile, kept, kept, squares],
            (factors, grad, panel, grad_v, weight, *scores[t], *tiles),
            limit,
            scratch=[pltpu.VMEM((cols, k), f32), pltpu.VMEM((k, k), f32), pack, across]
            + [pltpu.VMEM((cols, k), f32)] * (2 if last else 0),
            flops=8 * work, moved=4 * rows * cols,
        )
    tiles = summands(sums, "pb")
    return call(
        functools.partial(last_kernel, u_count, v_count),
        [tile, shape((each, k), f32)],
        (factors, grad, shifted(panel, "pb", 1), shifted(grad_v, "pb", 1), *tiles),
        limit,
    )


def solution(mesh):
    return jax.shard_map(
        lambda *args: tuple(per_device(*args)),
        mesh=mesh,
        in_specs=(P("pb", None), P(("pb", "dev"), None), P("pb"), P(), P()),
        out_specs=(P("pb", None), P(("pb", "dev"), None)),
        check_vma=False,
    )
```

```python
import functools

import jax
import jax.numpy as jnp
from jax import lax
from jax.experimental import pallas as pl
from jax.experimental.pallas import tpu as pltpu
from jax.sharding import PartitionSpec as P

STRATA = 3
epsilon = 1e-06
learning_rate = 0.3


HBM = pl.BlockSpec(memory_space=pltpu.HBM)
VMEM = pl.BlockSpec(memory_space=pltpu.VMEM)
f32, bf16 = jnp.float32, jnp.bfloat16


def dot(a, b):
    return jnp.dot(a, b, preferred_element_type=f32)


def pieces(x):
    hi = x.astype(bf16)
    return hi, (x - hi.astype(f32)).astype(bf16)


def call(kernel, out_shape, operands, *, limit, in_specs=None, scratch=(), flops=0, moved=0):
    return pl.pallas_call(
        kernel,
        out_shape=out_shape,
        in_specs=in_specs or [VMEM] * len(operands),
        out_specs=jax.tree.map(lambda _: VMEM, out_shape),
        scratch_shapes=list(scratch),
        compiler_params=pltpu.CompilerParams(vmem_limit_bytes=limit),
        cost_estimate=pl.CostEstimate(flops=flops, bytes_accessed=moved, transcendentals=0),
    )(*operands)


def wrapped(value):
    return jnp.int32((value + (1 << 31)) % (1 << 32) - (1 << 31))


def hash_block(base, first_ref, second_ref, col, width):
    rows = first_ref.shape[0]
    step = 32
    local_rows = lax.broadcasted_iota(jnp.int32, (step, width), 0)
    local_cols = lax.broadcasted_iota(jnp.int32, (step, width), 1)
    offsets = local_rows * 668265263 + local_cols * 1274126177 + base

    def down(mixed, count):
        return lax.shift_right_logical(mixed, jnp.full(mixed.shape, count, jnp.int32))

    for row in range(0, rows, step):
        mixed = offsets + wrapped(row * 668265263 + col * 1274126177)
        mixed = mixed ^ down(mixed, 15)
        mixed = mixed * 73244475
        mixed = mixed ^ down(mixed, 13)
        mixed = mixed * 1911520717
        mixed = mixed ^ down(mixed, 16)
        first_ref[pl.ds(row, step), pl.ds(col, width)] = (
            (mixed & 65280).astype(f32) - 32768.0
        ).astype(bf16)
        second_ref[pl.ds(row, step), pl.ds(col, width)] = (mixed & 255).astype(f32).astype(bf16)


def step_size(tiles, row, count):
    tile = functools.reduce(jnp.add, [ref[row : row + 8, :] for ref in tiles])
    return learning_rate / jnp.sqrt(
        jnp.sum(tile, axis=(0, 1), keepdims=True) / count + epsilon
    )


def times_gram(left, gram):
    k = gram.shape[0]
    high, low = pieces(gram)
    left_high, left_low = pieces(left)
    packed = jnp.concatenate([left_high, left_low], axis=1)
    wide = jnp.concatenate(
        [
            jnp.concatenate([high, low], axis=1),
            jnp.concatenate([high, jnp.zeros_like(low)], axis=1),
        ],
        axis=0,
    )
    out = dot(packed, wide)
    return out[:, :k] + out[:, k:]


def fold(square):
    k = square.shape[0] // 2
    return square[:k, :k] + (square[:k, k:] + square[k:, :k])


def add_squares(ref, row, block):
    rows, k = block.shape
    ref[row : row + 8, :] += jnp.sum((block * block).reshape(rows // 8, 8, k), axis=0)


def score_strip(packed_ref, first_ref, second_ref, at, *out_refs):
    k = out_refs[0].shape[1]
    out = dot(packed_ref[...], first_ref[:, at]) + dot(packed_ref[...], second_ref[:, at])
    for i, ref in enumerate(out_refs):
        ref[at, :] = (out[2 * i * k : (2 * i + 1) * k] + out[(2 * i + 1) * k : (2 * i + 2) * k]).T


def score_products(packed_ref, first_ref, second_ref, *out_refs):
    width = 256

    def strip(j, _):
        at = pl.ds(pl.multiple_of(j * width, width), width)
        score_strip(packed_ref, first_ref, second_ref, at, *out_refs)
        return 0

    lax.fori_loop(0, first_ref.shape[1] // width, strip, 0)


def across(weight, array):
    return jnp.concatenate(pieces((weight * array).T), axis=0)


def beside(array):
    return jnp.concatenate(pieces(array), axis=1)


down_scale = 1 / 32768


def spread_weight(row_ref, weight_ref):
    strips, k = row_ref.shape
    for i in range(strips):
        weight_ref[i * k : (i + 1) * k, :] = jnp.broadcast_to(row_ref[i : i + 1, :], (k, k)).T


def tile_base(plan_ref, seeds_ref, position, stratum, rows, cols):
    groups = plan_ref.shape[0]
    panel_id = plan_ref[lax.rem(position + (STRATA * groups - stratum), groups)]
    return (
        seeds_ref[position, panel_id] * 374761393
        + (position * rows) * 668265263
        + (panel_id * cols) * 1274126177
    )


def hash_and_products(base, packed_ref, first_ref, second_ref, *out_refs, held=None):
    width = 256
    for col in range(0, first_ref.shape[1], width):
        hash_block(base, first_ref, second_ref, col, width)
        if held is not None:
            score_strip(*held)
        held = (packed_ref, first_ref, second_ref, pl.ds(col, width), *out_refs)
    return held


def start_kernel(strata, *refs):
    ins, (weight_ref, gram_ref, bases_ref), refs = refs[:4], refs[4:7], refs[7:]
    tiles, refs = refs[: 3 * len(strata)], refs[3 * len(strata) :]
    plan_ref, seeds_ref, factors_ref, row_ref, packed_ref, sem = refs
    copies = [
        pltpu.make_async_copy(src, dst, sem.at[i])
        for i, (src, dst) in enumerate(zip(ins, (plan_ref, seeds_ref, factors_ref, row_ref)))
    ]
    for copy in copies:
        copy.start()
    for copy in copies:
        copy.wait()
    spread_weight(row_ref, weight_ref)
    rows, cols = tiles[0].shape
    factors = factors_ref[...]
    packed = across(weight_ref[...], factors)
    gram_ref[...] = fold(dot(packed, beside(factors)))
    packed_ref[...] = packed * jnp.asarray(down_scale, bf16)
    position = lax.axis_index("pb")
    groups = plan_ref.shape[0]
    other = lax.rem(position + groups - 1, groups)
    base_of = functools.partial(tile_base, plan_ref, seeds_ref)
    lanes = bases_ref.shape[1]
    bases_ref[...] = jnp.zeros_like(bases_ref)
    bases_ref[0:1, :] = jnp.full((1, lanes), base_of(position, STRATA - 1, rows, cols), jnp.int32)
    bases_ref[1:2, :] = jnp.full((1, lanes), base_of(other, 0, rows, cols), jnp.int32)
    held = None
    for t, first_ref, second_ref, p_ref in zip(strata, tiles[::3], tiles[1::3], tiles[2::3]):
        held = hash_and_products(
            base_of(position, t, rows, cols), packed_ref, first_ref, second_ref, p_ref, held=held
        )
    score_strip(*held)


def other_kernel(factors_ref, row_ref, bases_ref, p_ref, gram_ref,
                 weight_ref, packed_ref, first_ref, second_ref):
    spread_weight(row_ref, weight_ref)
    factors = factors_ref[...]
    packed = across(weight_ref[...], factors)
    gram_ref[...] = fold(dot(packed, beside(factors)))
    packed_ref[...] = packed * jnp.asarray(down_scale, bf16)
    score_strip(*hash_and_products(bases_ref[1:2, 0:1], packed_ref, first_ref, second_ref, p_ref))


def grad_terms(factors_ref, grad_ref, weight_ref, cross_ref, square_ref, packed_ref):
    packed = across(weight_ref[...], grad_ref[...])
    cross = fold(dot(packed, beside(factors_ref[...])))
    cross_ref[...] = cross + cross.T
    square_ref[...] = fold(dot(packed, beside(grad_ref[...])))
    packed_ref[...] = packed * jnp.asarray(down_scale, bf16)


def grad_kernel(factors_ref, grad_ref, weight_ref, first_ref, second_ref, sums_ref,
                p_ref, cross_ref, square_ref, packed_ref):
    grad_terms(factors_ref, grad_ref, weight_ref, cross_ref, square_ref, packed_ref)
    score_products(packed_ref, first_ref, second_ref, p_ref)


def late_kernel(factors_ref, grad_ref, weight_ref, bases_ref, sums_ref,
                p_ref, cross_ref, square_ref, p_factors_ref, gram_ref, first_ref, second_ref,
                packed_ref):
    k = p_ref.shape[1]
    grad_terms(factors_ref, grad_ref, weight_ref, cross_ref, square_ref, packed_ref.at[: 2 * k])
    other = across(weight_ref[...], factors_ref[...])
    gram_ref[...] = fold(dot(other, beside(factors_ref[...])))
    packed_ref[2 * k :, :] = other * jnp.asarray(down_scale, bf16)
    score_strip(*hash_and_products(
        bases_ref[0:1, 0:1], packed_ref, first_ref, second_ref, p_ref, p_factors_ref
    ))


def panel_side(panel, p, gram, h_ref, squares_ref, packed_ref, panel_gram_ref):
    h = p - times_gram(panel, gram)
    if h_ref is not None:
        h_ref[...] = h
    squares_ref[...] = jnp.zeros_like(squares_ref)
    add_squares(squares_ref, 0, h)
    packed = beside(panel)
    packed_ref[...] = packed * jnp.asarray(down_scale, bf16)
    panel_gram_ref[...] = fold(
        lax.dot_general(packed, packed, (((0,), (0,)), ((), ())), preferred_element_type=f32)
    )


def first_head_kernel(*refs):
    parts, refs = refs[:-7], refs[-7:]
    p_ref, gram_ref, _, panel_ref, squares_ref, packed_ref, panel_gram_ref = refs
    own = lax.axis_index("dev")
    each = parts[0].shape[0]
    for i, part in enumerate(parts):
        place = pl.multiple_of((own ^ i) * each, each) if len(parts) > 1 else 0
        panel_ref[pl.ds(place, each), :] = part[...]
    panel_side(panel_ref[...], p_ref[...], gram_ref[...], None, squares_ref, packed_ref,
               panel_gram_ref)


def head_kernel(last, u_count, v_count, *refs):
    u_before, g_before, v_before, h_before, pu_ref, pg_ref, uu_ref, ug_ref, gg_ref = refs[:9]
    at, rest = 9, 8 if last else 6
    h = h_before[...]
    if not last:
        at = 10
        h = h - times_gram(v_before[...], refs[9][...])
    tiles, refs = refs[at:-rest], refs[-rest:]
    factors_ref, v_out, h_out, squares_ref, packed_ref, panel_gram_ref = refs[:6]
    panel_ref, h_ref = refs[6:] if last else (v_out, h_out)
    step = step_size(tiles, 0, u_count)
    factors_ref[...] = u_before[...] + step * g_before[...]
    panel_ref[...] = v_before[...] + step_size(tiles, 8, v_count) * h
    gram = uu_ref[...] + step * (ug_ref[...] + step * gg_ref[...])
    panel_side(panel_ref[...], pu_ref[...] + step * pg_ref[...], gram, h_ref, squares_ref,
               packed_ref, panel_gram_ref)
    if last:
        each = v_out.shape[0]
        at = pl.ds(pl.multiple_of(lax.axis_index("dev") * each, each), each)
        v_out[...] = panel_ref[at, :]
        h_out[...] = h_ref[at, :]


def tail_kernel(factors_ref, weight_ref, first_ref, second_ref, packed_ref, panel_gram_ref,
                panel_squares_ref, grad_ref, squares_ref):
    rows, k = factors_ref.shape
    squares_ref[:8, :] = jnp.zeros((8, k), f32)
    squares_ref[8:, :] = panel_squares_ref[...]
    panel_gram = panel_gram_ref[...]
    height = 256

    def strip(j, _):
        at = pl.ds(pl.multiple_of(j * height, height), height)
        out = dot(first_ref[at, :], packed_ref[...]) + dot(second_ref[at, :], packed_ref[...])
        g = weight_ref[at, :] * (
            (out[:, :k] + out[:, k:]) - times_gram(factors_ref[at, :], panel_gram)
        )
        grad_ref[at, :] = g
        add_squares(squares_ref, 0, g)
        return 0

    lax.fori_loop(0, rows // height, strip, 0)


def last_kernel(u_count, v_count, u_ref, g_ref, v_ref, h_ref, *refs):
    tiles, (u_out, v_out) = refs[:-2], refs[-2:]
    u_out[...] = u_ref[...] + step_size(tiles, 0, u_count) * g_ref[...]
    v_out[...] = v_ref[...] + step_size(tiles, 8, v_count) * h_ref[...]


def shifted(array, axis, by):
    size = lax.axis_size(axis)
    return lax.ppermute(array, axis, [(i, (i + by) % size) for i in range(size)])


def crossed(array, axis, mask):
    return lax.ppermute(array, axis, [(i, i ^ mask) for i in range(lax.axis_size(axis))])


def power_of_two(size):
    return size & (size - 1) == 0


def summands(tile, axis):
    size = lax.axis_size(axis)
    if not power_of_two(size):
        return [lax.psum(tile, axis)]
    tiles, at = [tile], 1
    while at < size:
        tile = functools.reduce(jnp.add, tiles)
        span = 3 if at > 1 and 2 * at < size else 1
        tiles = [tile] + [crossed(tile, axis, at * i) for i in range(1, span + 1)]
        at *= span + 1
    return tiles


def per_device(query_factors, panel_factors, query_weight, plan, tile_seeds):
    groups = lax.axis_size("pb")
    spread = lax.axis_size("dev")
    rows, k = query_factors.shape
    each = panel_factors.shape[0]
    cols = each * spread
    u_count = float(rows * groups * k)
    v_count = float(cols * groups * k)
    shape = jax.ShapeDtypeStruct
    work = 2 * rows * cols * k
    limit = (8 << 20) + (8 if rows * cols <= 1 << 20 else 4) * rows * cols + 28 * k * (rows + cols)
    tile = shape((rows, k), f32)
    whole = shape((cols, k), f32)
    gram_of = shape((k, k), f32)
    pair = [shape((rows, cols), bf16)] * 2
    pack = shape((cols, 2 * k), bf16)
    squares = shape((8, k), f32)
    run = functools.partial(call, limit=limit, moved=4 * rows * cols)

    if spread <= 4 and power_of_two(spread):
        parts = [panel_factors] + [crossed(panel_factors, "dev", i) for i in range(1, spread)]
    else:
        parts = [lax.all_gather(panel_factors, "dev", axis=0, tiled=True)]

    row = query_weight.reshape(rows // k, k)
    factors_by = shifted(query_factors, "pb", 1)
    row_by = shifted(row, "pb", 1)
    across_of = pltpu.VMEM((2 * k, rows), bf16)
    pair_of = [pltpu.VMEM((rows, cols), bf16)] * 2

    def started(strata):
        return run(
            functools.partial(start_kernel, strata),
            [tile, gram_of, shape((8, k), jnp.int32)] + [*pair, whole] * len(strata),
            tuple(pltpu.with_memory_space_constraint(x, pltpu.HBM)
                  for x in (plan, tile_seeds, query_factors, row)),
            in_specs=[HBM] * 4,
            scratch=[pltpu.SMEM(plan.shape, jnp.int32), pltpu.SMEM(tile_seeds.shape, jnp.int32),
                     pltpu.VMEM((rows, k), f32), pltpu.VMEM((rows // k, k), f32),
                     across_of, pltpu.SemaphoreType.DMA((4,))],
            flops=6 * work,
        )

    if rows * cols <= 1 << 20:
        weight, gram, bases, *tiles_of = started([0, 1])
    else:
        weight, gram, bases, *tiles_of = started([0])
        tiles_of += started([1])[3:]
    first, second, p, first_next, second_next, p_factors = tiles_of
    factors = query_factors
    p_by, gram_by = run(
        other_kernel, [whole, gram_of], (factors_by, row_by, bases),
        scratch=[pltpu.VMEM((rows, k), f32), across_of, *pair_of], flops=4 * work,
    )
    panel, panel_squares, packed, panel_gram = run(
        first_head_kernel, [whole, squares, pack, gram_of], (*parts, p, gram, gram_by),
        flops=work // 2,
    )
    for t in range(STRATA):
        last = t == STRATA - 1
        panel = shifted(panel, "pb", 1)
        if t > 0:
            grad_v = shifted(grad_v, "pb", 1)
        grad, sums = run(
            tail_kernel, [tile, shape((16, k), f32)],
            (factors, weight, first, second, packed, panel_gram, panel_squares),
            flops=4 * work,
        )
        tiles = summands(sums, "pb")
        if last:
            break
        outs = [whole, gram_of, gram_of]
        if t == 0:
            first, second = first_next, second_next
            p_grad, cross, square = run(
                grad_kernel, outs, (factors, grad, weight, first, second, sums),
                scratch=[across_of], flops=4 * work,
            )
            step = (p_by,)
            more = (gram_by,)
        else:
            p_grad, cross, square, p_factors, gram, first, second = run(
                late_kernel, outs + [whole, gram_of, *pair],
                (factors, grad, weight, bases, sums),
                scratch=[pltpu.VMEM((4 * k, rows), bf16)], flops=8 * work,
            )
            step = (grad_v,)
            more = ()
        ends = t + 1 == STRATA - 1
        kept = shape((each, k), f32) if ends else whole
        factors, panel, grad_v, panel_squares, packed, panel_gram = run(
            functools.partial(head_kernel, ends, u_count, v_count),
            [tile, kept, kept, squares, pack, gram_of],
            (factors, grad, panel, *step, p_factors, p_grad, gram, cross, square, *more, *tiles),
            scratch=[pltpu.VMEM((cols, k), f32)] * (2 if ends else 0), flops=work // 2,
        )
    return run(
        functools.partial(last_kernel, u_count, v_count),
        [tile, shape((each, k), f32)],
        (factors, grad, panel, grad_v, *tiles),
    )


def solution(mesh):
    return jax.shard_map(
        lambda *args: tuple(per_device(*args)),
        mesh=mesh,
        in_specs=(P("pb", None), P(("pb", "dev"), None), P("pb"), P(), P()),
        out_specs=(P("pb", None), P(("pb", "dev"), None)),
        check_vma=False,
    )
```

```python
import functools

import jax
import jax.numpy as jnp
from jax import lax
from jax.experimental import pallas as pl
from jax.experimental.pallas import tpu as pltpu
from jax.sharding import PartitionSpec as P

STRATA = 3
epsilon = 1e-06
learning_rate = 0.3


HBM = pl.BlockSpec(memory_space=pltpu.HBM)
VMEM = pl.BlockSpec(memory_space=pltpu.VMEM)
f32, bf16 = jnp.float32, jnp.bfloat16


def dot(a, b):
    return jnp.dot(a, b, preferred_element_type=f32)


def pieces(x):
    hi = x.astype(bf16)
    return hi, (x - hi.astype(f32)).astype(bf16)


def call(kernel, out_shape, operands, *, limit, in_specs=None, scratch=(), flops=0, moved=0):
    return pl.pallas_call(
        kernel,
        out_shape=out_shape,
        in_specs=in_specs or [VMEM] * len(operands),
        out_specs=jax.tree.map(lambda _: VMEM, out_shape),
        scratch_shapes=list(scratch),
        compiler_params=pltpu.CompilerParams(vmem_limit_bytes=limit),
        cost_estimate=pl.CostEstimate(flops=flops, bytes_accessed=moved, transcendentals=0),
    )(*operands)


def wrapped(value):
    return jnp.int32((value + (1 << 31)) % (1 << 32) - (1 << 31))


def hash_block(base, first_ref, second_ref, col, width):
    rows = first_ref.shape[0]
    step = 32
    local_rows = lax.broadcasted_iota(jnp.int32, (step, width), 0)
    local_cols = lax.broadcasted_iota(jnp.int32, (step, width), 1)
    offsets = local_rows * 668265263 + local_cols * 1274126177 + base

    def down(mixed, count):
        return lax.shift_right_logical(mixed, jnp.full(mixed.shape, count, jnp.int32))

    for row in range(0, rows, step):
        mixed = offsets + wrapped(row * 668265263 + col * 1274126177)
        mixed = mixed ^ down(mixed, 15)
        mixed = mixed * 73244475
        mixed = mixed ^ down(mixed, 13)
        mixed = mixed * 1911520717
        mixed = mixed ^ down(mixed, 16)
        first_ref[pl.ds(row, step), pl.ds(col, width)] = (
            (mixed & 65280).astype(f32) - 32768.0
        ).astype(bf16)
        second_ref[pl.ds(row, step), pl.ds(col, width)] = (mixed & 255).astype(f32).astype(bf16)


def step_size(tiles, row, count):
    tile = functools.reduce(jnp.add, [ref[row : row + 8, :] for ref in tiles])
    return learning_rate / jnp.sqrt(
        jnp.sum(tile, axis=(0, 1), keepdims=True) / count + epsilon
    )


def times_gram(left, gram):
    k = gram.shape[0]
    high, low = pieces(gram)
    left_high, left_low = pieces(left)
    packed = jnp.concatenate([left_high, left_low], axis=1)
    wide = jnp.concatenate(
        [
            jnp.concatenate([high, low], axis=1),
            jnp.concatenate([high, jnp.zeros_like(low)], axis=1),
        ],
        axis=0,
    )
    out = dot(packed, wide)
    return out[:, :k] + out[:, k:]


def fold(square):
    k = square.shape[0] // 2
    return square[:k, :k] + (square[:k, k:] + square[k:, :k])


def add_squares(ref, row, block):
    rows, k = block.shape
    ref[row : row + 8, :] += jnp.sum((block * block).reshape(rows // 8, 8, k), axis=0)


def score_strip(packed_ref, first_ref, second_ref, at, *out_refs):
    k = out_refs[0].shape[1]
    out = dot(packed_ref[...], first_ref[:, at]) + dot(packed_ref[...], second_ref[:, at])
    for i, ref in enumerate(out_refs):
        ref[at, :] = (out[2 * i * k : (2 * i + 1) * k] + out[(2 * i + 1) * k : (2 * i + 2) * k]).T


def steps(count, body):
    if count <= 4:
        for j in range(count):
            body(j)
    else:
        lax.fori_loop(0, count, lambda j, _: (body(j), 0)[1], 0)


def score_products(packed_ref, first_ref, second_ref, *out_refs):
    width = 256

    def strip(j):
        at = pl.ds(j * width if isinstance(j, int) else pl.multiple_of(j * width, width), width)
        score_strip(packed_ref, first_ref, second_ref, at, *out_refs)

    steps(first_ref.shape[1] // width, strip)


def across(weight, array):
    return jnp.concatenate(pieces((weight * array).T), axis=0)


def beside(array):
    return jnp.concatenate(pieces(array), axis=1)


down_scale = 1 / 32768


def spread_weight(row_ref, weight_ref):
    strips, k = row_ref.shape
    for i in range(strips):
        weight_ref[i * k : (i + 1) * k, :] = jnp.broadcast_to(row_ref[i : i + 1, :], (k, k)).T


def tile_base(plan_ref, seeds_ref, position, stratum, rows, cols):
    groups = plan_ref.shape[0]
    panel_id = plan_ref[lax.rem(position + (STRATA * groups - stratum), groups)]
    return (
        seeds_ref[position, panel_id] * 374761393
        + (position * rows) * 668265263
        + (panel_id * cols) * 1274126177
    )


def hash_and_products(base, packed_ref, first_ref, second_ref, *out_refs, start=0, held=None):
    width = 256
    for col in range(start, first_ref.shape[1], width):
        hash_block(base, first_ref, second_ref, col, width)
        if held is not None:
            score_strip(*held)
        held = (packed_ref, first_ref, second_ref, pl.ds(col, width), *out_refs)
    return held


def start_kernel(strata, *refs):
    ins, (weight_ref, gram_ref, bases_ref), refs = refs[:4], refs[4:7], refs[7:]
    tiles, refs = refs[: 3 * len(strata)], refs[3 * len(strata) :]
    plan_ref, seeds_ref, factors_ref, row_ref, packed_ref, sem = refs
    copies = [
        pltpu.make_async_copy(src, dst, sem.at[i])
        for i, (src, dst) in enumerate(zip(ins, (plan_ref, seeds_ref, factors_ref, row_ref)))
    ]
    for copy in copies:
        copy.start()
    rows, cols = tiles[0].shape
    position = lax.axis_index("pb")
    groups = plan_ref.shape[0]
    other = lax.rem(position + groups - 1, groups)
    base_of = functools.partial(tile_base, plan_ref, seeds_ref)
    for copy in copies[:2]:
        copy.wait()
    hash_block(base_of(position, strata[0], rows, cols), *tiles[:2], 0, 256)
    for copy in copies[2:]:
        copy.wait()
    spread_weight(row_ref, weight_ref)
    factors = factors_ref[...]
    packed = across(weight_ref[...], factors)
    gram_ref[...] = fold(dot(packed, beside(factors)))
    packed_ref[...] = packed * jnp.asarray(down_scale, bf16)
    lanes = bases_ref.shape[1]
    bases_ref[...] = jnp.zeros_like(bases_ref)
    bases_ref[0:1, :] = jnp.full((1, lanes), base_of(position, STRATA - 1, rows, cols), jnp.int32)
    bases_ref[1:2, :] = jnp.full((1, lanes), base_of(other, 0, rows, cols), jnp.int32)
    held = (packed_ref, *tiles[:2], pl.ds(0, 256), tiles[2])
    for t, first_ref, second_ref, p_ref in zip(strata, tiles[::3], tiles[1::3], tiles[2::3]):
        held = hash_and_products(
            base_of(position, t, rows, cols), packed_ref, first_ref, second_ref, p_ref,
            start=256 if t == strata[0] else 0, held=held,
        )
    score_strip(*held)


def other_kernel(factors_ref, row_ref, bases_ref, p_ref, gram_ref,
                 weight_ref, packed_ref, first_ref, second_ref):
    base = bases_ref[1:2, 0:1]
    hash_block(base, first_ref, second_ref, 0, 256)
    spread_weight(row_ref, weight_ref)
    factors = factors_ref[...]
    packed = across(weight_ref[...], factors)
    gram_ref[...] = fold(dot(packed, beside(factors)))
    packed_ref[...] = packed * jnp.asarray(down_scale, bf16)
    score_strip(*hash_and_products(
        base, packed_ref, first_ref, second_ref, p_ref, start=256,
        held=(packed_ref, first_ref, second_ref, pl.ds(0, 256), p_ref),
    ))


def grad_terms(factors_ref, grad_ref, weight_ref, cross_ref, square_ref, packed_ref):
    packed = across(weight_ref[...], grad_ref[...])
    cross = fold(dot(packed, beside(factors_ref[...])))
    cross_ref[...] = cross + cross.T
    square_ref[...] = fold(dot(packed, beside(grad_ref[...])))
    packed_ref[...] = packed * jnp.asarray(down_scale, bf16)


def grad_kernel(factors_ref, grad_ref, weight_ref, first_ref, second_ref, sums_ref,
                p_ref, cross_ref, square_ref, packed_ref):
    grad_terms(factors_ref, grad_ref, weight_ref, cross_ref, square_ref, packed_ref)
    score_products(packed_ref, first_ref, second_ref, p_ref)


def late_kernel(factors_ref, grad_ref, weight_ref, bases_ref, sums_ref,
                p_ref, cross_ref, square_ref, p_factors_ref, gram_ref, first_ref, second_ref,
                packed_ref):
    k = p_ref.shape[1]
    grad_terms(factors_ref, grad_ref, weight_ref, cross_ref, square_ref, packed_ref.at[: 2 * k])
    other = across(weight_ref[...], factors_ref[...])
    gram_ref[...] = fold(dot(other, beside(factors_ref[...])))
    packed_ref[2 * k :, :] = other * jnp.asarray(down_scale, bf16)
    score_strip(*hash_and_products(
        bases_ref[0:1, 0:1], packed_ref, first_ref, second_ref, p_ref, p_factors_ref
    ))


def panel_side(panel, p, gram, h_ref, squares_ref, packed_ref, panel_gram_ref):
    h = p - times_gram(panel, gram)
    if h_ref is not None:
        h_ref[...] = h
    squares_ref[...] = jnp.zeros_like(squares_ref)
    add_squares(squares_ref, 0, h)
    packed = beside(panel)
    packed_ref[...] = packed * jnp.asarray(down_scale, bf16)
    panel_gram_ref[...] = fold(
        lax.dot_general(packed, packed, (((0,), (0,)), ((), ())), preferred_element_type=f32)
    )


def first_head_kernel(*refs):
    parts, refs = refs[:-7], refs[-7:]
    p_ref, gram_ref, _, panel_ref, squares_ref, packed_ref, panel_gram_ref = refs
    own = lax.axis_index("dev")
    each = parts[0].shape[0]
    for i, part in enumerate(parts):
        place = pl.multiple_of((own ^ i) * each, each) if len(parts) > 1 else 0
        panel_ref[pl.ds(place, each), :] = part[...]
    panel_side(panel_ref[...], p_ref[...], gram_ref[...], None, squares_ref, packed_ref,
               panel_gram_ref)


def carry_kernel(v_count, v_ref, p_ref, gram_ref, *refs):
    tiles, panel_ref = refs[:-1], refs[-1]
    v = v_ref[...]
    panel_ref[...] = v + step_size(tiles, 8, v_count) * (p_ref[...] - times_gram(v, gram_ref[...]))


def head_kernel(last, u_count, v_count, *refs):
    u_before, g_before, v_before, h_before, pu_ref, pg_ref, uu_ref, ug_ref, gg_ref = refs[:9]
    rest = 8 if last else 5
    tiles, refs = refs[9:-rest], refs[-rest:]
    if last:
        factors_ref, v_out, h_out, squares_ref, packed_ref, panel_gram_ref, panel_ref, h_ref = refs
    else:
        factors_ref, h_ref, squares_ref, packed_ref, panel_gram_ref = refs
        panel_ref = v_before
    step = step_size(tiles, 0, u_count)
    factors_ref[...] = u_before[...] + step * g_before[...]
    if last:
        panel_ref[...] = v_before[...] + step_size(tiles, 8, v_count) * h_before[...]
    gram = uu_ref[...] + step * (ug_ref[...] + step * gg_ref[...])
    panel_side(panel_ref[...], pu_ref[...] + step * pg_ref[...], gram, h_ref, squares_ref,
               packed_ref, panel_gram_ref)
    if last:
        each = v_out.shape[0]
        at = pl.ds(pl.multiple_of(lax.axis_index("dev") * each, each), each)
        v_out[...] = panel_ref[at, :]
        h_out[...] = h_ref[at, :]


def tail_kernel(factors_ref, weight_ref, first_ref, second_ref, packed_ref, panel_gram_ref,
                panel_squares_ref, grad_ref, squares_ref):
    rows, k = factors_ref.shape
    squares_ref[:8, :] = jnp.zeros((8, k), f32)
    squares_ref[8:, :] = panel_squares_ref[...]
    panel_gram = panel_gram_ref[...]
    height = 256

    def strip(j):
        at = pl.ds(j * height if isinstance(j, int) else pl.multiple_of(j * height, height), height)
        out = dot(first_ref[at, :], packed_ref[...]) + dot(second_ref[at, :], packed_ref[...])
        g = weight_ref[at, :] * (
            (out[:, :k] + out[:, k:]) - times_gram(factors_ref[at, :], panel_gram)
        )
        grad_ref[at, :] = g
        add_squares(squares_ref, 0, g)

    steps(rows // height, strip)


def last_kernel(u_count, v_count, u_ref, g_ref, v_ref, h_ref, *refs):
    tiles, (u_out, v_out) = refs[:-2], refs[-2:]
    u_out[...] = u_ref[...] + step_size(tiles, 0, u_count) * g_ref[...]
    v_out[...] = v_ref[...] + step_size(tiles, 8, v_count) * h_ref[...]


def shifted(array, axis, by):
    size = lax.axis_size(axis)
    return lax.ppermute(array, axis, [(i, (i + by) % size) for i in range(size)])


def crossed(array, axis, mask):
    return lax.ppermute(array, axis, [(i, i ^ mask) for i in range(lax.axis_size(axis))])


def power_of_two(size):
    return size & (size - 1) == 0


def summands(tile, axis):
    size = lax.axis_size(axis)
    if not power_of_two(size):
        return [lax.psum(tile, axis)]
    tiles, at = [tile], 1
    while at < size:
        tile = functools.reduce(jnp.add, tiles)
        span = 3 if at > 1 and 2 * at < size else 1
        tiles = [tile] + [crossed(tile, axis, at * i) for i in range(1, span + 1)]
        at *= span + 1
    return tiles


def per_device(query_factors, panel_factors, query_weight, plan, tile_seeds):
    groups = lax.axis_size("pb")
    spread = lax.axis_size("dev")
    rows, k = query_factors.shape
    each = panel_factors.shape[0]
    cols = each * spread
    u_count = float(rows * groups * k)
    v_count = float(cols * groups * k)
    shape = jax.ShapeDtypeStruct
    work = 2 * rows * cols * k
    limit = (8 << 20) + (8 if rows * cols <= 1 << 20 else 4) * rows * cols + 28 * k * (rows + cols)
    tile = shape((rows, k), f32)
    whole = shape((cols, k), f32)
    gram_of = shape((k, k), f32)
    pair = [shape((rows, cols), bf16)] * 2
    pack = shape((cols, 2 * k), bf16)
    squares = shape((8, k), f32)
    run = functools.partial(call, limit=limit, moved=4 * rows * cols)

    if spread <= 4 and power_of_two(spread):
        parts = [panel_factors] + [crossed(panel_factors, "dev", i) for i in range(1, spread)]
    else:
        parts = [lax.all_gather(panel_factors, "dev", axis=0, tiled=True)]

    row = query_weight.reshape(rows // k, k)
    factors_by = shifted(query_factors, "pb", 1)
    row_by = shifted(row, "pb", 1)
    across_of = pltpu.VMEM((2 * k, rows), bf16)
    pair_of = [pltpu.VMEM((rows, cols), bf16)] * 2

    def started(strata):
        return run(
            functools.partial(start_kernel, strata),
            [tile, gram_of, shape((8, k), jnp.int32)] + [*pair, whole] * len(strata),
            tuple(pltpu.with_memory_space_constraint(x, pltpu.HBM)
                  for x in (plan, tile_seeds, query_factors, row)),
            in_specs=[HBM] * 4,
            scratch=[pltpu.SMEM(plan.shape, jnp.int32), pltpu.SMEM(tile_seeds.shape, jnp.int32),
                     pltpu.VMEM((rows, k), f32), pltpu.VMEM((rows // k, k), f32),
                     across_of, pltpu.SemaphoreType.DMA((4,))],
            flops=6 * work,
        )

    if rows * cols <= 1 << 20:
        weight, gram, bases, *tiles_of = started([0, 1])
    else:
        weight, gram, bases, *tiles_of = started([0])
        tiles_of += started([1])[3:]
    first, second, p, first_next, second_next, p_factors = tiles_of
    factors = query_factors
    p_by, gram_by = run(
        other_kernel, [whole, gram_of], (factors_by, row_by, bases),
        scratch=[pltpu.VMEM((rows, k), f32), across_of, *pair_of], flops=4 * work,
    )
    panel, panel_squares, packed, panel_gram = run(
        first_head_kernel, [whole, squares, pack, gram_of], (*parts, p, gram, gram_by),
        flops=work // 2,
    )
    for t in range(STRATA):
        last = t == STRATA - 1
        panel = shifted(panel, "pb", 1)
        if t > 0:
            grad_v = shifted(grad_v, "pb", 1)
        grad, sums = run(
            tail_kernel, [tile, shape((16, k), f32)],
            (factors, weight, first, second, packed, panel_gram, panel_squares),
            flops=4 * work,
        )
        tiles = summands(sums, "pb")
        if last:
            break
        outs = [whole, gram_of, gram_of]
        if t == 0:
            first, second = first_next, second_next
            p_grad, cross, square = run(
                grad_kernel, outs, (factors, grad, weight, first, second, sums),
                scratch=[across_of], flops=4 * work,
            )
            (panel,) = run(
                functools.partial(carry_kernel, v_count), [whole],
                (panel, p_by, gram_by, *tiles), flops=work // 8,
            )
            kept, grad_v = [], gram_by
        else:
            p_grad, cross, square, p_factors, gram, first, second = run(
                late_kernel, outs + [whole, gram_of, *pair],
                (factors, grad, weight, bases, sums),
                scratch=[pltpu.VMEM((4 * k, rows), bf16)], flops=8 * work,
            )
            kept = [shape((each, k), f32)]
        ends = t > 0
        factors, *held, grad_v, panel_squares, packed, panel_gram = run(
            functools.partial(head_kernel, ends, u_count, v_count),
            [tile, *kept, kept[0] if ends else whole, squares, pack, gram_of],
            (factors, grad, panel, grad_v, p_factors, p_grad, gram, cross, square, *tiles),
            scratch=[pltpu.VMEM((cols, k), f32)] * (2 if ends else 0), flops=work // 2,
        )
        panel = held[0] if ends else panel
    return run(
        functools.partial(last_kernel, u_count, v_count),
        [tile, shape((each, k), f32)],
        (factors, grad, panel, grad_v, *tiles),
    )


def solution(mesh):
    return jax.shard_map(
        lambda *args: tuple(per_device(*args)),
        mesh=mesh,
        in_specs=(P("pb", None), P(("pb", "dev"), None), P("pb"), P(), P()),
        out_specs=(P("pb", None), P(("pb", "dev"), None)),
        check_vma=False,
    )
```

```python
import functools

import jax
import jax.numpy as jnp
from jax import lax
from jax.experimental import pallas as pl
from jax.experimental.pallas import tpu as pltpu
from jax.sharding import PartitionSpec as P

STRATA = 3
epsilon = 1e-06
learning_rate = 0.3


HBM = pl.BlockSpec(memory_space=pltpu.HBM)
VMEM = pl.BlockSpec(memory_space=pltpu.VMEM)
f32, bf16 = jnp.float32, jnp.bfloat16


def dot(a, b):
    return jnp.dot(a, b, preferred_element_type=f32)


def pieces(x):
    hi = x.astype(bf16)
    return hi, (x - hi.astype(f32)).astype(bf16)


def call(kernel, out_shape, operands, *, limit, in_specs=None, scratch=(), flops=0, moved=0):
    return pl.pallas_call(
        kernel,
        out_shape=out_shape,
        in_specs=in_specs or [VMEM] * len(operands),
        out_specs=jax.tree.map(lambda _: VMEM, out_shape),
        scratch_shapes=list(scratch),
        compiler_params=pltpu.CompilerParams(vmem_limit_bytes=limit),
        cost_estimate=pl.CostEstimate(flops=flops, bytes_accessed=moved, transcendentals=0),
    )(*operands)


def wrapped(value):
    return jnp.int32((value + (1 << 31)) % (1 << 32) - (1 << 31))


def hash_block(base, first_ref, second_ref, col, width):
    rows = first_ref.shape[0]
    step = 32
    local_rows = lax.broadcasted_iota(jnp.int32, (step, width), 0)
    local_cols = lax.broadcasted_iota(jnp.int32, (step, width), 1)
    offsets = local_rows * 668265263 + local_cols * 1274126177 + base

    def down(mixed, count):
        return lax.shift_right_logical(mixed, jnp.full(mixed.shape, count, jnp.int32))

    for row in range(0, rows, step):
        mixed = offsets + wrapped(row * 668265263 + col * 1274126177)
        mixed = mixed ^ down(mixed, 15)
        mixed = mixed * 73244475
        mixed = mixed ^ down(mixed, 13)
        mixed = mixed * 1911520717
        mixed = mixed ^ down(mixed, 16)
        first_ref[pl.ds(row, step), pl.ds(col, width)] = (
            (mixed & 65280).astype(f32) - 32768.0
        ).astype(bf16)
        second_ref[pl.ds(row, step), pl.ds(col, width)] = (mixed & 255).astype(f32).astype(bf16)


def step_size(tiles, row, count):
    tile = functools.reduce(jnp.add, [ref[row : row + 8, :] for ref in tiles])
    return learning_rate / jnp.sqrt(
        jnp.sum(tile, axis=(0, 1), keepdims=True) / count + epsilon
    )


def times_gram(left, gram):
    k = gram.shape[0]
    high, low = pieces(gram)
    left_high, left_low = pieces(left)
    packed = jnp.concatenate([left_high, left_low], axis=1)
    wide = jnp.concatenate(
        [
            jnp.concatenate([high, low], axis=1),
            jnp.concatenate([high, jnp.zeros_like(low)], axis=1),
        ],
        axis=0,
    )
    out = dot(packed, wide)
    return out[:, :k] + out[:, k:]


def fold(square):
    k = square.shape[0] // 2
    return square[:k, :k] + (square[:k, k:] + square[k:, :k])


def add_squares(ref, row, block):
    rows, k = block.shape
    ref[row : row + 8, :] += jnp.sum((block * block).reshape(rows // 8, 8, k), axis=0)


def score_strip(packed_ref, first_ref, second_ref, at, *out_refs):
    k = out_refs[0].shape[1]
    out = dot(packed_ref[...], first_ref[:, at]) + dot(packed_ref[...], second_ref[:, at])
    for i, ref in enumerate(out_refs):
        ref[at, :] = (out[2 * i * k : (2 * i + 1) * k] + out[(2 * i + 1) * k : (2 * i + 2) * k]).T


def steps(count, body):
    if count <= 4:
        for j in range(count):
            body(j)
    else:
        lax.fori_loop(0, count, lambda j, _: (body(j), 0)[1], 0)


def score_products(packed_ref, first_ref, second_ref, *out_refs):
    width = 256

    def strip(j):
        at = pl.ds(j * width if isinstance(j, int) else pl.multiple_of(j * width, width), width)
        score_strip(packed_ref, first_ref, second_ref, at, *out_refs)

    steps(first_ref.shape[1] // width, strip)


def across(weight, array):
    return jnp.concatenate(pieces((weight * array).T), axis=0)


def beside(array):
    return jnp.concatenate(pieces(array), axis=1)


down_scale = 1 / 32768


def spread_weight(row_ref, weight_ref):
    strips, k = row_ref.shape
    for i in range(strips):
        weight_ref[i * k : (i + 1) * k, :] = jnp.broadcast_to(row_ref[i : i + 1, :], (k, k)).T


def tile_base(plan_ref, seeds_ref, position, stratum, rows, cols):
    groups = plan_ref.shape[0]
    panel_id = plan_ref[lax.rem(position + (STRATA * groups - stratum), groups)]
    return (
        seeds_ref[position, panel_id] * 374761393
        + (position * rows) * 668265263
        + (panel_id * cols) * 1274126177
    )


def hash_and_products(base, packed_ref, first_ref, second_ref, *out_refs, start=0, held=None):
    width = 256
    for col in range(start, first_ref.shape[1], width):
        hash_block(base, first_ref, second_ref, col, width)
        if held is not None:
            score_strip(*held)
        held = (packed_ref, first_ref, second_ref, pl.ds(col, width), *out_refs)
    return held


def start_kernel(strata, *refs):
    ins, (weight_ref, gram_ref, bases_ref), refs = refs[:4], refs[4:7], refs[7:]
    tiles, refs = refs[: 3 * len(strata)], refs[3 * len(strata) :]
    plan_ref, seeds_ref, factors_ref, row_ref, packed_ref, sem = refs
    copies = [
        pltpu.make_async_copy(src, dst, sem.at[i])
        for i, (src, dst) in enumerate(zip(ins, (plan_ref, seeds_ref, factors_ref, row_ref)))
    ]
    for copy in copies:
        copy.start()
    rows, cols = tiles[0].shape
    position = lax.axis_index("pb")
    groups = plan_ref.shape[0]
    other = lax.rem(position + groups - 1, groups)
    base_of = functools.partial(tile_base, plan_ref, seeds_ref)
    for copy in copies[:2]:
        copy.wait()
    hash_block(base_of(position, strata[0], rows, cols), *tiles[:2], 0, 256)
    for copy in copies[2:]:
        copy.wait()
    spread_weight(row_ref, weight_ref)
    factors = factors_ref[...]
    packed = across(weight_ref[...], factors)
    gram_ref[...] = fold(dot(packed, beside(factors)))
    packed_ref[...] = packed * jnp.asarray(down_scale, bf16)
    lanes = bases_ref.shape[1]
    bases_ref[...] = jnp.zeros_like(bases_ref)
    bases_ref[0:1, :] = jnp.full((1, lanes), base_of(position, STRATA - 1, rows, cols), jnp.int32)
    bases_ref[1:2, :] = jnp.full((1, lanes), base_of(other, 0, rows, cols), jnp.int32)
    held = (packed_ref, *tiles[:2], pl.ds(0, 256), tiles[2])
    for t, first_ref, second_ref, p_ref in zip(strata, tiles[::3], tiles[1::3], tiles[2::3]):
        held = hash_and_products(
            base_of(position, t, rows, cols), packed_ref, first_ref, second_ref, p_ref,
            start=256 if t == strata[0] else 0, held=held,
        )
    score_strip(*held)


def other_kernel(factors_ref, row_ref, bases_ref, p_ref, gram_ref,
                 weight_ref, packed_ref, first_ref, second_ref):
    base = bases_ref[1:2, 0:1]
    hash_block(base, first_ref, second_ref, 0, 256)
    spread_weight(row_ref, weight_ref)
    factors = factors_ref[...]
    packed = across(weight_ref[...], factors)
    gram_ref[...] = fold(dot(packed, beside(factors)))
    packed_ref[...] = packed * jnp.asarray(down_scale, bf16)
    score_strip(*hash_and_products(
        base, packed_ref, first_ref, second_ref, p_ref, start=256,
        held=(packed_ref, first_ref, second_ref, pl.ds(0, 256), p_ref),
    ))


def grad_terms(factors_ref, grad_ref, weight_ref, cross_ref, square_ref, packed_ref):
    packed = across(weight_ref[...], grad_ref[...])
    cross = fold(dot(packed, beside(factors_ref[...])))
    cross_ref[...] = cross + cross.T
    square_ref[...] = fold(dot(packed, beside(grad_ref[...])))
    packed_ref[...] = packed * jnp.asarray(down_scale, bf16)


def grad_kernel(factors_ref, grad_ref, weight_ref, first_ref, second_ref, sums_ref,
                p_ref, cross_ref, square_ref, packed_ref):
    grad_terms(factors_ref, grad_ref, weight_ref, cross_ref, square_ref, packed_ref)
    score_products(packed_ref, first_ref, second_ref, p_ref)


def late_kernel(factors_ref, grad_ref, weight_ref, bases_ref, sums_ref,
                p_ref, cross_ref, square_ref, p_factors_ref, gram_ref, first_ref, second_ref,
                packed_ref):
    k = p_ref.shape[1]
    grad_terms(factors_ref, grad_ref, weight_ref, cross_ref, square_ref, packed_ref.at[: 2 * k])
    other = across(weight_ref[...], factors_ref[...])
    gram_ref[...] = fold(dot(other, beside(factors_ref[...])))
    packed_ref[2 * k :, :] = other * jnp.asarray(down_scale, bf16)
    score_strip(*hash_and_products(
        bases_ref[0:1, 0:1], packed_ref, first_ref, second_ref, p_ref, p_factors_ref
    ))


def panel_side(panel, p, gram, h_ref, squares_ref, packed_ref, panel_gram_ref):
    h = p - times_gram(panel, gram)
    if h_ref is not None:
        h_ref[...] = h
    squares_ref[...] = jnp.zeros_like(squares_ref)
    add_squares(squares_ref, 0, h)
    packed = beside(panel)
    packed_ref[...] = packed * jnp.asarray(down_scale, bf16)
    panel_gram_ref[...] = fold(
        lax.dot_general(packed, packed, (((0,), (0,)), ((), ())), preferred_element_type=f32)
    )


def first_head_kernel(*refs):
    parts, refs = refs[:-7], refs[-7:]
    p_ref, gram_ref, _, panel_ref, squares_ref, packed_ref, panel_gram_ref = refs
    own = lax.axis_index("dev")
    each = parts[0].shape[0]
    for i, part in enumerate(parts):
        place = pl.multiple_of((own ^ i) * each, each) if len(parts) > 1 else 0
        panel_ref[pl.ds(place, each), :] = part[...]
    panel_side(panel_ref[...], p_ref[...], gram_ref[...], None, squares_ref, packed_ref,
               panel_gram_ref)


def carry_kernel(v_count, v_ref, p_ref, gram_ref, *refs):
    tiles, panel_ref = refs[:-1], refs[-1]
    v = v_ref[...]
    panel_ref[...] = v + step_size(tiles, 8, v_count) * (p_ref[...] - times_gram(v, gram_ref[...]))


def head_kernel(last, u_count, v_count, *refs):
    u_before, g_before, v_before, h_before, pu_ref, pg_ref, uu_ref, ug_ref, gg_ref = refs[:9]
    rest = 7 if last else 5
    tiles, refs = refs[9:-rest], refs[-rest:]
    if last:
        factors_ref, out_ref, squares_ref, packed_ref, panel_gram_ref, panel_ref, h_ref = refs
    else:
        factors_ref, h_ref, squares_ref, packed_ref, panel_gram_ref = refs
        panel_ref = v_before
    step = step_size(tiles, 0, u_count)
    factors_ref[...] = u_before[...] + step * g_before[...]
    if last:
        panel_ref[...] = v_before[...] + step_size(tiles, 8, v_count) * h_before[...]
    gram = uu_ref[...] + step * (ug_ref[...] + step * gg_ref[...])
    panel_side(panel_ref[...], pu_ref[...] + step * pg_ref[...], gram, h_ref, squares_ref,
               packed_ref, panel_gram_ref)
    if last:
        each = out_ref.shape[0] // 2
        at = pl.ds(pl.multiple_of(lax.axis_index("dev") * each, each), each)
        out_ref[:each, :] = panel_ref[at, :]
        out_ref[each:, :] = h_ref[at, :]


def tail_kernel(factors_ref, weight_ref, first_ref, second_ref, packed_ref, panel_gram_ref,
                panel_squares_ref, grad_ref, squares_ref):
    rows, k = factors_ref.shape
    squares_ref[:8, :] = jnp.zeros((8, k), f32)
    squares_ref[8:, :] = panel_squares_ref[...]
    panel_gram = panel_gram_ref[...]
    height = 256

    def strip(j):
        at = pl.ds(j * height if isinstance(j, int) else pl.multiple_of(j * height, height), height)
        out = dot(first_ref[at, :], packed_ref[...]) + dot(second_ref[at, :], packed_ref[...])
        g = weight_ref[at, :] * (
            (out[:, :k] + out[:, k:]) - times_gram(factors_ref[at, :], panel_gram)
        )
        grad_ref[at, :] = g
        add_squares(squares_ref, 0, g)

    steps(rows // height, strip)


def last_kernel(u_count, v_count, u_ref, g_ref, both_ref, *refs):
    tiles, (u_out, v_out) = refs[:-2], refs[-2:]
    u_out[...] = u_ref[...] + step_size(tiles, 0, u_count) * g_ref[...]
    each = v_out.shape[0]
    v_out[...] = both_ref[:each, :] + step_size(tiles, 8, v_count) * both_ref[each:, :]


def shifted(array, axis, by):
    size = lax.axis_size(axis)
    return lax.ppermute(array, axis, [(i, (i + by) % size) for i in range(size)])


def crossed(array, axis, mask):
    return lax.ppermute(array, axis, [(i, i ^ mask) for i in range(lax.axis_size(axis))])


def power_of_two(size):
    return size & (size - 1) == 0


def summands(tile, axis):
    size = lax.axis_size(axis)
    if not power_of_two(size):
        return [lax.psum(tile, axis)]
    tiles, at = [tile], 1
    while at < size:
        tile = functools.reduce(jnp.add, tiles)
        span = 3 if at > 1 and 2 * at < size else 1
        tiles = [tile] + [crossed(tile, axis, at * i) for i in range(1, span + 1)]
        at *= span + 1
    return tiles


def per_device(query_factors, panel_factors, query_weight, plan, tile_seeds):
    groups = lax.axis_size("pb")
    spread = lax.axis_size("dev")
    rows, k = query_factors.shape
    each = panel_factors.shape[0]
    cols = each * spread
    u_count = float(rows * groups * k)
    v_count = float(cols * groups * k)
    shape = jax.ShapeDtypeStruct
    work = 2 * rows * cols * k
    limit = (8 << 20) + (8 if rows * cols <= 1 << 20 else 4) * rows * cols + 28 * k * (rows + cols)
    tile = shape((rows, k), f32)
    whole = shape((cols, k), f32)
    gram_of = shape((k, k), f32)
    pair = [shape((rows, cols), bf16)] * 2
    pack = shape((cols, 2 * k), bf16)
    squares = shape((8, k), f32)
    run = functools.partial(call, limit=limit, moved=4 * rows * cols)

    if spread <= 4 and power_of_two(spread):
        parts = [panel_factors] + [crossed(panel_factors, "dev", i) for i in range(1, spread)]
    else:
        parts = [lax.all_gather(panel_factors, "dev", axis=0, tiled=True)]

    row = query_weight.reshape(rows // k, k)
    factors_by = shifted(query_factors, "pb", 1)
    row_by = shifted(row, "pb", 1)
    across_of = pltpu.VMEM((2 * k, rows), bf16)
    pair_of = [pltpu.VMEM((rows, cols), bf16)] * 2

    def started(strata):
        return run(
            functools.partial(start_kernel, strata),
            [tile, gram_of, shape((8, k), jnp.int32)] + [*pair, whole] * len(strata),
            tuple(pltpu.with_memory_space_constraint(x, pltpu.HBM)
                  for x in (plan, tile_seeds, query_factors, row)),
            in_specs=[HBM] * 4,
            scratch=[pltpu.SMEM(plan.shape, jnp.int32), pltpu.SMEM(tile_seeds.shape, jnp.int32),
                     pltpu.VMEM((rows, k), f32), pltpu.VMEM((rows // k, k), f32),
                     across_of, pltpu.SemaphoreType.DMA((4,))],
            flops=6 * work,
        )

    if rows * cols <= 1 << 20:
        weight, gram, bases, *tiles_of = started([0, 1])
    else:
        weight, gram, bases, *tiles_of = started([0])
        tiles_of += started([1])[3:]
    first, second, p, first_next, second_next, p_factors = tiles_of
    factors = query_factors
    p_by, gram_by = run(
        other_kernel, [whole, gram_of], (factors_by, row_by, bases),
        scratch=[pltpu.VMEM((rows, k), f32), across_of, *pair_of], flops=4 * work,
    )
    panel, panel_squares, packed, panel_gram = run(
        first_head_kernel, [whole, squares, pack, gram_of], (*parts, p, gram, gram_by),
        flops=work // 2,
    )
    for t in range(STRATA):
        last = t == STRATA - 1
        panel = shifted(panel, "pb", 1)
        if 0 < t < STRATA - 1:
            grad_v = shifted(grad_v, "pb", 1)
        grad, sums = run(
            tail_kernel, [tile, shape((16, k), f32)],
            (factors, weight, first, second, packed, panel_gram, panel_squares),
            flops=4 * work,
        )
        tiles = summands(sums, "pb")
        if last:
            break
        outs = [whole, gram_of, gram_of]
        if t == 0:
            first, second = first_next, second_next
            p_grad, cross, square = run(
                grad_kernel, outs, (factors, grad, weight, first, second, sums),
                scratch=[across_of], flops=4 * work,
            )
            (panel,) = run(
                functools.partial(carry_kernel, v_count), [whole],
                (panel, p_by, gram_by, *tiles), flops=work // 8,
            )
            grad_v = gram_by
        else:
            p_grad, cross, square, p_factors, gram, first, second = run(
                late_kernel, outs + [whole, gram_of, *pair],
                (factors, grad, weight, bases, sums),
                scratch=[pltpu.VMEM((4 * k, rows), bf16)], flops=8 * work,
            )
        ends = t > 0
        factors, moving, panel_squares, packed, panel_gram = run(
            functools.partial(head_kernel, ends, u_count, v_count),
            [tile, shape((2 * each, k), f32) if ends else whole, squares, pack, gram_of],
            (factors, grad, panel, grad_v, p_factors, p_grad, gram, cross, square, *tiles),
            scratch=[pltpu.VMEM((cols, k), f32)] * (2 if ends else 0), flops=work // 2,
        )
        if ends:
            panel = moving
        else:
            grad_v = moving
    return run(
        functools.partial(last_kernel, u_count, v_count),
        [tile, shape((each, k), f32)],
        (factors, grad, panel, *tiles),
    )


def solution(mesh):
    return jax.shard_map(
        lambda *args: tuple(per_device(*args)),
        mesh=mesh,
        in_specs=(P("pb", None), P(("pb", "dev"), None), P("pb"), P(), P()),
        out_specs=(P("pb", None), P(("pb", "dev"), None)),
        check_vma=False,
    )
```
